512 devices in a mesh: req: 64 (over x, y, core), kv: 8 (over z).
Axes of the slice: x: 4, y: 8, z: 8, core: 2. Of those that a mesh axis runs over, the one named last changes fastest.
Arguments:
- tokens: bfloat16 [64, 4096], P('req'), may hold values from -6 to 6
- attn_gain: float32 [4096], replicated, may hold values from 0.5 to 1.5
- mlp_gain: float32 [4096], replicated, may hold values from 0.5 to 1.5
- w_query: bfloat16 [4096, 4096], P('req', 'kv'), may hold values from -0.09375 to 0.09375
- w_key: bfloat16 [4096, 1024], P('req', 'kv'), may hold values from -0.09375 to 0.09375
- w_value: bfloat16 [4096, 1024], P('req', 'kv'), may hold values from -0.09375 to 0.09375
- w_out: bfloat16 [4096, 4096], P('kv', 'req'), may hold values from -0.09375 to 0.09375
- w_gate: bfloat16 [4096, 14336], P('kv', 'req'), may hold values from -0.09375 to 0.09375
- w_up: bfloat16 [4096, 14336], P('kv', 'req'), may hold values from -0.09375 to 0.09375
- w_down: bfloat16 [14336, 4096], P('req', 'kv'), may hold values from -0.046875 to 0.046875
- cache_keys: bfloat16 [1024, 256, 1024], P('req', None, 'kv')
- cache_values: bfloat16 [1024, 256, 1024], P('req', None, 'kv'), may hold values from -6 to 6
- slot_owner: int32 [1024], P('req'), may hold values from 0 to 63, as said below
- slot_fill: int32 [1024], P('req'), may hold values from 0 to 256, as said below
Outputs:
- out: bfloat16 [64, 4096], P('req', 'kv')
The draws below stay inside these ranges and needn't reach their ends.
Inputs may be any that keep to these rules, and one draw needn't show every extreme that they name: `slot_owner`: every request owns one slot or more. `slot_fill`: every index of req holds one full slot and one empty slot.
All inputs are finite; a program needn't handle non-finite values.
Results may differ from the reference program's by a relative error of at most 0.013.
The reference program's roundings to bfloat16 on the way (of `normed`, `prob_low`, `heads`, `normed2` and `hidden`) count: a program that leaves them out, or rounds other values in their place, can miss the bound.
Values may be sent and summed in bfloat16 or wider, within the bound.
A program may use at most 64 MiB of HBM per device.

```python
import jax
import jax.numpy as jnp
from jax import lax

D = 4096
HQ = 32
HK = 8
DH = 128
FF = 14336
SLOTS = 16
BLK = 256
REQUESTS = 64
SLOTS_ALL = 1024
N_REQ = 64


def slot_table(key):
    first = jax.random.randint(jax.random.fold_in(key, 11), (SLOTS_ALL,), 0, REQUESTS)
    second = jax.random.randint(jax.random.fold_in(key, 12), (SLOTS_ALL,), 0, REQUESTS)
    order = jax.random.permutation(jax.random.fold_in(key, 13), REQUESTS).astype(jnp.int32)
    place = jnp.arange(SLOTS_ALL, dtype=jnp.int32)
    owner = jnp.where(place < REQUESTS, order[place % REQUESTS], order[jnp.minimum(first, second)])
    filled = jax.random.randint(jax.random.fold_in(key, 14), (SLOTS_ALL,), 0, BLK + 1)
    filled = jnp.where(place % SLOTS == 0, BLK, filled)
    filled = jnp.where(place % SLOTS == 1, 0, filled)
    return (owner.astype(jnp.int32), filled.astype(jnp.int32))


def draw_slot_owner(key, part):
    return slot_table(key)[0]


def draw_slot_fill(key, part):
    return slot_table(key)[1]


def draw_cache_keys(key, part):
    base = jax.random.normal(jax.random.fold_in(key, 21), (SLOTS_ALL, BLK, HK * DH), jnp.float32)
    return base.astype(jnp.bfloat16)


def steps_of(rng, shape, split, smallest, largest):
    factor_of = 1.0
    for dim, shards_of in split:
        steps = jax.random.uniform(jax.random.fold_in(jax.random.fold_in(rng, 6), dim), (shards_of,), jnp.float32, smallest / len(split), largest / len(split))
        factor_of = factor_of * jnp.repeat(jnp.exp(steps), shape[dim] // shards_of).reshape((-1,) + (1,) * (len(shape) - 1 - dim))
    return factor_of


def scatter_about(key, extent, spread, reach, shards=(), kind=jnp.bfloat16):
    result = jax.random.normal(key, extent, jnp.float32) * spread
    if len(shards) > 0:
        result = steps_of(key, extent, shards, -0.22, 0.18) * result
    return jnp.clip(result, min=-reach, max=reach).astype(kind)


def setup_inputs(seed: int = 0) -> dict:
    seeds = jax.random.split(jax.random.key(seed), 15)
    return {
        "tokens": scatter_about(seeds[0], (REQUESTS, D), 1.0, 6.0, ((0, 64),)),
        "attn_gain": jnp.clip(1.0 + 0.1 * jax.random.normal(seeds[1], (D,), jnp.float32), 0.5, 1.5),
        "mlp_gain": jnp.clip(1.0 + 0.1 * jax.random.normal(seeds[2], (D,), jnp.float32), 0.5, 1.5),
        "w_query": scatter_about(seeds[3], (D, HQ * DH), D ** -0.5, 0.09375, ((0, 64), (1, 8))),
        "w_key": scatter_about(seeds[4], (D, HK * DH), D ** -0.5, 0.09375, ((0, 64), (1, 8))),
        "w_value": scatter_about(seeds[5], (D, HK * DH), D ** -0.5, 0.09375, ((0, 64), (1, 8))),
        "w_out": scatter_about(seeds[6], (HQ * DH, D), (HQ * DH) ** -0.5, 0.09375, ((0, 8), (1, 64))),
        "w_gate": scatter_about(seeds[7], (D, FF), D ** -0.5, 0.09375, ((0, 8), (1, 64))),
        "w_up": scatter_about(seeds[8], (D, FF), D ** -0.5, 0.09375, ((0, 8), (1, 64))),
        "w_down": scatter_about(seeds[9], (FF, D), FF ** -0.5, 0.046875, ((0, 64), (1, 8))),
        "cache_keys": draw_cache_keys(jax.random.fold_in(seeds[14], 71), 0),
        "cache_values": scatter_about(seeds[11], (SLOTS_ALL, BLK, HK * DH), 1.0, 6.0, ((0, 64), (2, 8))),
        "slot_owner": draw_slot_owner(jax.random.fold_in(seeds[14], 71), 0),
        "slot_fill": draw_slot_fill(jax.random.fold_in(seeds[14], 71), 0),
    }


EPS = 1e-05
NEG = -1e+30

def rms_norm(rows, gain):
    mean = lax.optimization_barrier(jnp.mean(rows * rows, axis=-1, keepdims=True))
    return (rows * lax.rsqrt(mean + EPS) * gain).astype(jnp.bfloat16)

def reference(tokens, attn_gain, mlp_gain, w_query, w_key, w_value, w_out, w_gate, w_up, w_down, cache_keys, cache_values, slot_owner, slot_fill):
    group = HQ // HK
    scale = DH ** (-0.5)
    resid_in = tokens.astype(jnp.float32)
    normed = rms_norm(resid_in, attn_gain)
    query = jnp.dot(normed, w_query, preferred_element_type=jnp.float32).astype(jnp.bfloat16).reshape(REQUESTS, HK, group, DH)
    new_key = jnp.dot(normed, w_key, preferred_element_type=jnp.float32).astype(jnp.bfloat16).reshape(REQUESTS, HK, DH)
    new_value = jnp.dot(normed, w_value, preferred_element_type=jnp.float32).astype(jnp.bfloat16).reshape(REQUESTS, HK, DH)
    keys_all = cache_keys.reshape(N_REQ, SLOTS, BLK, HK, DH)
    values_all = cache_values.reshape(N_REQ, SLOTS, BLK, HK, DH)
    owners = slot_owner.reshape(N_REQ, SLOTS).astype(jnp.int32)
    fills = slot_fill.reshape(N_REQ, SLOTS).astype(jnp.int32)

    def device_slots(packed):
        key_block, value_block, owned, filled = packed
        slot_query = jnp.take(query, owned, axis=0).astype(jnp.float32)
        scores = jnp.einsum('skgd,sbkd->skgb', slot_query, key_block.astype(jnp.float32)) * scale
        valid = (jnp.arange(BLK, dtype=jnp.int32)[None, :] < filled[:, None])[:, None, None, :]
        masked = jnp.where(valid, scores, NEG)
        slot_max = lax.optimization_barrier(jnp.max(masked, axis=-1))
        prob = jnp.where(valid, jnp.exp(masked - slot_max[..., None]), 0.0)
        slot_total = lax.optimization_barrier(jnp.sum(prob, axis=-1))
        prob_low = lax.optimization_barrier(prob.astype(jnp.bfloat16)).astype(jnp.float32)
        slot_acc = jnp.einsum('skgb,sbkd->skgd', prob_low, value_block.astype(jnp.float32))
        return (slot_max, slot_total, slot_acc)
    slot_max, slot_total, slot_acc = lax.map(device_slots, (keys_all, values_all, owners, fills))
    slot_max = slot_max.reshape(SLOTS_ALL, HK, group)
    slot_total = slot_total.reshape(SLOTS_ALL, HK, group)
    slot_acc = slot_acc.reshape(SLOTS_ALL, HK, group, DH)
    flat_owner = slot_owner.astype(jnp.int32)
    run_max = jnp.full((REQUESTS, HK, group), NEG, jnp.float32).at[flat_owner].max(slot_max)
    rescale = jnp.exp(slot_max - run_max[flat_owner])
    run_total = jnp.zeros((REQUESTS, HK, group), jnp.float32).at[flat_owner].add(slot_total * rescale)
    run_acc = jnp.zeros((REQUESTS, HK, group, DH), jnp.float32).at[flat_owner].add(slot_acc * rescale[..., None])
    own_score = lax.optimization_barrier(jnp.sum(query.astype(jnp.float32) * new_key.astype(jnp.float32)[:, :, None, :], axis=-1)) * scale
    highest = jnp.maximum(run_max, own_score)
    older = jnp.exp(run_max - highest)
    fresh = jnp.exp(own_score - highest)
    total = run_total * older + fresh
    accum = run_acc * older[..., None] + fresh[..., None] * new_value.astype(jnp.float32)[:, :, None, :]
    heads = (accum / total[..., None]).astype(jnp.bfloat16).reshape(REQUESTS, HQ * DH)
    resid = resid_in + jnp.dot(heads, w_out, preferred_element_type=jnp.float32)
    normed2 = rms_norm(resid, mlp_gain)
    gate = jnp.dot(normed2, w_gate, preferred_element_type=jnp.float32)
    up_part = jnp.dot(normed2, w_up, preferred_element_type=jnp.float32)
    hidden = (jax.nn.silu(gate) * up_part).astype(jnp.bfloat16)
    return (resid + jnp.dot(hidden, w_down, preferred_element_type=jnp.float32)).astype(jnp.bfloat16)
```

```python
import jax
import jax.numpy as jnp
from jax import lax
from jax.sharding import PartitionSpec as P

HQ = 32
HK = 8
DH = 128


EPS = 1e-05
NEG = -1e30


def scatter_sum(rows, axis):
    parts = lax.all_to_all(rows, axis, split_axis=0, concat_axis=0, tiled=True)
    devices = lax.axis_size(axis)
    return jnp.sum(parts.reshape((devices, -1) + parts.shape[1:]), axis=0)


def spread(row, axis):
    devices = lax.axis_size(axis)
    copies = jnp.broadcast_to(row[None], (devices,) + row.shape)
    parts = lax.all_to_all(copies, axis, split_axis=0, concat_axis=0, tiled=True)
    return parts.reshape((devices * row.shape[0],) + row.shape[1:])


def rms_norm(rows, gain):
    mean = jnp.mean(rows * rows, axis=-1, keepdims=True)
    return (rows * lax.rsqrt(mean + EPS) * gain).astype(jnp.bfloat16)


def merge_parts(parts, group):
    acc = parts[:, : group * DH].reshape(-1, group, DH)
    part_max = parts[:, group * DH : group * DH + group]
    part_total = parts[:, group * DH + group : group * DH + 2 * group]
    highest = jnp.max(part_max, axis=0)
    share = jnp.exp(part_max - highest)
    return highest, jnp.sum(part_total * share, axis=0), jnp.sum(acc * share[..., None], axis=0)


def finish_heads(run_max, run_total, run_acc, query, new_key, new_value, scale):
    own_score = (
        jnp.sum(query.astype(jnp.float32) * new_key.astype(jnp.float32)[:, :, None, :], axis=-1)
        * scale
    )
    highest = jnp.maximum(run_max, own_score)
    older = jnp.exp(run_max - highest)
    fresh = jnp.exp(own_score - highest)
    total = run_total * older + fresh
    accum = (
        run_acc * older[..., None] + fresh[..., None] * new_value.astype(jnp.float32)[:, :, None, :]
    )
    return (accum / total[..., None]).astype(jnp.bfloat16).reshape(query.shape[0], -1)


def per_device(
    tokens,
    attn_gain,
    mlp_gain,
    w_query,
    w_key,
    w_value,
    w_out,
    w_gate,
    w_up,
    w_down,
    cache_keys,
    cache_values,
    slot_owner,
    slot_fill,
):
    req_count = lax.axis_size("req")
    kv_count = lax.axis_size("kv")
    local_rows = tokens.shape[0]
    requests = local_rows * req_count
    group = HQ // HK
    kv_local = cache_keys.shape[2] // DH
    scale = DH ** (-0.5)
    resid_in = tokens.astype(jnp.float32)
    normed = rms_norm(resid_in, attn_gain)
    feature_cols = lax.all_to_all(normed, "req", split_axis=1, concat_axis=0, tiled=True)
    joined = jnp.concatenate([w_query, w_key, w_value], axis=1)
    width_q = w_query.shape[1]
    width_k = w_key.shape[1]
    partial_proj = jnp.dot(feature_cols, joined, preferred_element_type=jnp.float32)
    projected = scatter_sum(partial_proj, "req").astype(jnp.bfloat16)
    own_query = projected[:, :width_q]
    new_key = projected[:, width_q : width_q + width_k].reshape(local_rows, kv_local, DH)
    new_value = projected[:, width_q + width_k :].reshape(local_rows, kv_local, DH)
    query = spread(own_query, "req").reshape(requests, kv_local, group, DH)
    slots = cache_keys.shape[0]
    block_len = cache_keys.shape[1]
    keys_four = cache_keys.reshape(slots, block_len, kv_local, DH)
    values_four = cache_values.reshape(slots, block_len, kv_local, DH)
    slot_query = jnp.take(query, slot_owner, axis=0)
    scores = (
        jnp.einsum("skgd,sbkd->skgb", slot_query, keys_four, preferred_element_type=jnp.float32)
        * scale
    )
    valid = (lax.broadcasted_iota(jnp.int32, (slots, block_len), 1) < slot_fill[:, None])[
        :, None, None, :
    ]
    masked = jnp.where(valid, scores, NEG)
    slot_max = jnp.max(masked, axis=-1)
    prob = jnp.where(valid, jnp.exp(masked - slot_max[..., None]), 0.0)
    slot_total = jnp.sum(prob, axis=-1)
    slot_acc = jnp.einsum(
        "skgb,sbkd->skgd",
        prob.astype(jnp.bfloat16),
        values_four,
        preferred_element_type=jnp.float32,
    )
    run_max = jnp.full((requests, kv_local, group), NEG, jnp.float32).at[slot_owner].max(slot_max)
    rescale = jnp.exp(slot_max - run_max[slot_owner])
    run_total = (
        jnp.zeros((requests, kv_local, group), jnp.float32).at[slot_owner].add(slot_total * rescale)
    )
    run_acc = (
        jnp.zeros((requests, kv_local, group, DH), jnp.float32)
        .at[slot_owner]
        .add(slot_acc * rescale[..., None])
    )
    packed = jnp.concatenate(
        [
            run_acc.reshape(requests, group * DH),
            run_max.reshape(requests, group),
            run_total.reshape(requests, group),
            jnp.zeros((requests, DH - 2 * group), jnp.float32),
        ],
        axis=1,
    )
    parts = lax.all_to_all(packed, "req", split_axis=0, concat_axis=0, tiled=True)
    merged_max, merged_total, merged_acc = merge_parts(parts, group)
    own_heads = finish_heads(
        merged_max[None, None],
        merged_total[None, None],
        merged_acc[None, None],
        own_query.reshape(local_rows, kv_local, group, DH),
        new_key,
        new_value,
        scale,
    )
    heads = spread(own_heads, "req")
    out_part = jnp.dot(heads, w_out, preferred_element_type=jnp.float32)
    attn_part = lax.all_to_all(out_part, "req", split_axis=0, concat_axis=1, tiled=True)
    attn_rows = jnp.sum(spread(attn_part, "kv"), axis=0, keepdims=True)
    resid = resid_in + attn_rows
    normed2 = rms_norm(resid, mlp_gain)
    feature_width = normed2.shape[1] // kv_count
    kv_start = lax.axis_index("kv") * feature_width
    feature_block = lax.dynamic_slice_in_dim(normed2, kv_start, feature_width, 1)
    gate_up = jnp.concatenate([w_gate, w_up], axis=1)
    both_parts = jnp.dot(
        spread(feature_block, "req"),
        gate_up,
        preferred_element_type=jnp.float32,
    )
    both_sums = lax.all_to_all(
        both_parts.astype(jnp.bfloat16), "kv", split_axis=0, concat_axis=0, tiled=True
    )
    both_sums = jnp.sum(
        both_sums.reshape(kv_count, requests // kv_count, -1).astype(jnp.float32), axis=0
    )
    hidden_width = w_gate.shape[1]
    hidden = (jax.nn.silu(both_sums[:, :hidden_width]) * both_sums[:, hidden_width:]).astype(
        jnp.bfloat16
    )
    down_parts = jnp.dot(
        spread(hidden, "kv"), w_down, preferred_element_type=jnp.float32
    )
    down_home = scatter_sum(down_parts, "req")
    resid_block = lax.dynamic_slice_in_dim(resid, kv_start, feature_width, 1)
    return (resid_block + down_home).astype(jnp.bfloat16)


def solution(mesh):
    placed = (
        P("req", None),
        P(),
        P(),
        P("req", "kv"),
        P("req", "kv"),
        P("req", "kv"),
        P("kv", "req"),
        P("kv", "req"),
        P("kv", "req"),
        P("req", "kv"),
        P("req", None, "kv"),
        P("req", None, "kv"),
        P("req"),
        P("req"),
    )
    return jax.shard_map(
        per_device, mesh=mesh, in_specs=placed, out_specs=P("req", "kv"), check_vma=False
    )
```

```python
import jax
import jax.numpy as jnp
from jax import lax
from jax.experimental import pallas as pl
from jax.experimental.pallas import tpu as pltpu
from jax.sharding import PartitionSpec as P

HQ = 32
HK = 8
DH = 128
GROUP = HQ // HK
PAD = 8

EPS = 1e-05
NEG = -1e30
MESH = pl.DeviceIdType.MESH
F32 = jnp.float32
BF16 = jnp.bfloat16


def dot(left, right):
    return jnp.dot(left, right, preferred_element_type=F32)


def exchange_start(axis, me, count, source, landing, send_sem, recv_sem):
    @pl.loop(1, count)
    def _(step):
        peer = lax.rem(me + step, count)
        pltpu.make_async_remote_copy(
            src_ref=source(peer),
            dst_ref=landing.at[me],
            send_sem=send_sem,
            recv_sem=recv_sem,
            device_id={axis: peer},
            device_id_type=MESH,
        ).start()

    pltpu.make_async_copy(source(me), landing.at[me], recv_sem).start()


def landed(landing, recv_sem):
    pltpu.make_async_copy(landing, landing, recv_sem).wait()


def sent(landing, count, send_sem):
    view = landing.at[pl.ds(0, count - 1)]
    pltpu.make_async_copy(view, view, send_sem).wait()


def one_row(block):
    turned = pltpu.roll(block, 64, 1)
    low = lax.broadcasted_iota(jnp.int32, (1, 128), 1) < 64
    pairs = [
        jnp.where(low, block[2 * i : 2 * i + 1], turned[2 * i + 1 : 2 * i + 2]) for i in range(4)
    ]
    return jnp.concatenate(pairs, axis=1)


def layer_kernel(
    req_count,
    kv_count,
    owner_ref,
    fill_ref,
    tok_ref,
    again_ref,
    mgain_ref,
    wq_hbm,
    wk_hbm,
    wv_hbm,
    wo_hbm,
    wg_hbm,
    wu_hbm,
    wd_hbm,
    keys_hbm,
    values_hbm,
    out_ref,
    wq,
    wk,
    wv,
    wo,
    wg,
    wu,
    wd,
    keys,
    values,
    s1,
    l1,
    s2,
    l2,
    s3,
    l3,
    s4,
    l4,
    s5,
    l5,
    s6,
    l6,
    s7,
    l7,
    s8,
    l8,
    s9,
    l9,
    s10,
    l10,
    s11,
    l11,
    load_sem,
    send_sem,
    recv_sem,
):
    req = lax.axis_index("req")
    kv = lax.axis_index("kv")
    slots = keys.shape[0]
    block_len = keys.shape[1]
    scale = DH ** (-0.5)
    features = req_count * 64

    barrier = pltpu.get_barrier_semaphore()

    @pl.loop(1, req_count)
    def _(step):
        pl.semaphore_signal(
            barrier,
            inc=1,
            device_id={"req": lax.rem(req + step, req_count)},
            device_id_type=MESH,
        )

    @pl.loop(1, kv_count)
    def _(step):
        pl.semaphore_signal(
            barrier,
            inc=1,
            device_id={"kv": lax.rem(kv + step, kv_count)},
            device_id_type=MESH,
        )

    loads = [
        pltpu.make_async_copy(source, target, load_sem.at[i])
        for i, (source, target) in enumerate(
            [
                (wq_hbm, wq),
                (wk_hbm, wk),
                (wv_hbm, wv),
                (keys_hbm, keys),
                (values_hbm, values),
                (wo_hbm, wo),
                (wg_hbm, wg),
                (wu_hbm, wu),
                (wd_hbm, wd),
            ]
        )
    ]
    for load in loads:
        load.start()

    def req_start(i, source, landing):
        exchange_start("req", req, req_count, source, landing, send_sem.at[i], recv_sem.at[i])

    def kv_start(i, source, landing):
        exchange_start("kv", kv, kv_count, source, landing, send_sem.at[i], recv_sem.at[i])

    def kv_rows(array):
        return lambda peer: array.at[pl.ds(pl.multiple_of(peer * 8, 8), 8)]

    tok = tok_ref[...]
    mean = jnp.sum(jnp.sum(tok * tok, axis=1, keepdims=True), axis=0, keepdims=True) / features
    normed = (tok * lax.rsqrt(mean + EPS) * again_ref[...]).astype(BF16).astype(F32)
    s1[:, 0, :] = normed

    pl.semaphore_wait(barrier, req_count - 1 + kv_count - 1)

    req_start(0, lambda peer: s1.at[peer], l1)
    for load in loads[:3]:
        load.wait()
    landed(l1, recv_sem.at[0])
    columns = l1[:, 0, :][:, :64].astype(BF16)
    width_q = wq.shape[1]
    s2[:, 0, :] = jnp.concatenate(
        [dot(columns, wq[...]), dot(columns, wk[...]), dot(columns, wv[...])], axis=1
    )
    req_start(1, lambda peer: s2.at[peer], l2)
    landed(l2, recv_sem.at[1])
    projected = jnp.sum(l2[...], axis=0).astype(BF16).astype(F32)
    own_query = [projected[:, g * DH : (g + 1) * DH] for g in range(GROUP)]
    new_key = projected[:, width_q : width_q + DH]
    new_value = projected[:, width_q + DH : width_q + 2 * DH]
    for g in range(GROUP):
        s3[g : g + 1, :] = own_query[g]
    req_start(2, lambda peer: s3, l3)
    for load in loads[3:5]:
        load.wait()
    landed(l3, recv_sem.at[2])

    pos = lax.broadcasted_iota(jnp.int32, (PAD, block_len), 1)
    scores = []
    valid = []
    lane = lax.broadcasted_iota(jnp.int32, (1, slots * PAD), 1)
    slot_key = jnp.zeros((1, slots * PAD), jnp.int32)
    for s in range(slots):
        query = l3[owner_ref[s]]
        query = jnp.concatenate([query, jnp.zeros((PAD - GROUP, DH), F32)], axis=0).astype(BF16)
        scores.append(
            lax.dot_general(
                query, keys[s], (((1,), (1,)), ((), ())), preferred_element_type=F32
            )
        )
        valid.append(jnp.where(pos < fill_ref[s], 1.0, 0.0))
        slot_key = jnp.where(lane // PAD == s, owner_ref[s], slot_key)
    valid = jnp.concatenate(valid, axis=0) > 0.5
    masked = jnp.where(valid, jnp.concatenate(scores, axis=0) * scale, NEG)
    slot_max = jnp.max(masked, axis=1, keepdims=True)
    prob = jnp.where(valid, jnp.exp(masked - slot_max), 0.0)
    slot_total = jnp.sum(prob, axis=1, keepdims=True)
    prob_low = prob.astype(BF16)
    slot_acc = jnp.concatenate(
        [dot(prob_low[s * PAD : (s + 1) * PAD], values[s]) for s in range(slots)], axis=0
    )
    rows = slots * PAD
    slot_side = jnp.concatenate([slot_acc, jnp.broadcast_to(slot_total, (rows, DH))], axis=1)
    max_lane = jnp.transpose(jnp.broadcast_to(slot_max, (rows, rows)))[0:1]
    request = lax.broadcasted_iota(jnp.int32, (req_count, rows), 0)
    extra_lane = lax.broadcasted_iota(jnp.int32, (req_count, DH), 1)
    extra = jnp.zeros((req_count, DH), F32)
    for g in range(GROUP):
        mine = (request == slot_key) & (lane % PAD == g)
        part_max = jnp.max(jnp.where(mine, max_lane, NEG), axis=1, keepdims=True)
        weight = jnp.where(mine, jnp.exp(jnp.where(mine, max_lane, NEG) - part_max), 0.0)
        part = jnp.dot(
            weight, slot_side, preferred_element_type=F32, precision=lax.Precision.HIGHEST
        )
        s4[:, 0, g * DH : (g + 1) * DH] = part[:, :DH]
        extra = jnp.where(extra_lane == 2 * g, part[:, DH:], extra)
        extra = jnp.where(extra_lane == 2 * g + 1, part_max, extra)
    s4[:, 0, GROUP * DH :] = extra
    req_start(3, lambda peer: s4.at[peer], l4)
    landed(l4, recv_sem.at[3])

    extra = l4[:, 0, GROUP * DH :]
    for g in range(GROUP):
        part_total = extra[:, 2 * g : 2 * g + 1]
        part_max = extra[:, 2 * g + 1 : 2 * g + 2]
        run_max = jnp.max(part_max, axis=0, keepdims=True)
        share = jnp.exp(part_max - run_max)
        run_total = jnp.sum(part_total * share, axis=0, keepdims=True)
        run_acc = jnp.sum(l4[:, 0, g * DH : (g + 1) * DH] * share, axis=0, keepdims=True)
        own_score = jnp.sum(own_query[g] * new_key, axis=1, keepdims=True) * scale
        highest = jnp.maximum(run_max, own_score)
        older = jnp.exp(run_max - highest)
        fresh = jnp.exp(own_score - highest)
        total = run_total * older + fresh
        heads = (run_acc * older + fresh * new_value) / total
        s5[:, g * DH : (g + 1) * DH] = heads.astype(BF16).astype(F32)
    req_start(4, lambda peer: s5, l5)
    loads[5].wait()
    landed(l5, recv_sem.at[4])

    out_part = dot(l5[:, 0, :].astype(BF16), wo[...])
    s6[:, 0, :] = jnp.concatenate([out_part, jnp.zeros((req_count, 64), F32)], axis=1)
    req_start(5, lambda peer: s6.at[peer], l6)
    landed(l6, recv_sem.at[5])
    s7[...] = l6[:, 0, :]
    kv_start(6, kv_rows(s7), l7)
    landed(l7, recv_sem.at[6])
    block = pl.ds(pl.multiple_of(kv * 8, 8), 8)
    resid = tok_ref[block, :] + jnp.sum(l7[...], axis=0)
    squares = jnp.sum(jnp.sum(resid * resid, axis=1, keepdims=True), axis=0, keepdims=True)
    resid_row = one_row(resid)
    s8[:, :512] = one_row(resid * mgain_ref[block, :])
    s8[:, 512:] = jnp.broadcast_to(squares, (1, 128))
    req_start(7, lambda peer: s8, l8)
    for load in loads[6:8]:
        load.wait()
    landed(l8, recv_sem.at[7])

    scaled = l8[:, 0, :512].astype(BF16)
    width = wg.shape[1]
    s9[:, 128:256] = l8[:, 0, 512:]
    s9[:, :width] = dot(scaled, wg[...])
    s9[:, 384:512] = jnp.zeros((req_count, 128), F32)
    s9[:, 256 : 256 + width] = dot(scaled, wu[...])
    kv_start(8, kv_rows(s9), l9)
    landed(l9, recv_sem.at[8])
    both = jnp.sum(l9[...], axis=0)
    factor = lax.rsqrt(both[:, 255:256] / features + EPS)
    gate = both[:, :256] * factor
    up = both[:, 256:] * factor
    hidden = (gate / (1.0 + jnp.exp(-gate)) * up).astype(BF16).astype(F32)
    s10[...] = hidden
    kv_start(9, lambda peer: s10, l10)
    loads[8].wait()
    landed(l10, recv_sem.at[9])
    units = l10[...].reshape(req_count, 256)[:, :width].astype(BF16)
    s11[:, 0, :] = dot(units, wd[...])
    req_start(10, lambda peer: s11.at[peer], l11)
    landed(l11, recv_sem.at[10])
    out_ref[...] = (resid_row + jnp.sum(l11[...], axis=0)).astype(BF16)

    for i, landing in enumerate([l1, l2, l3, l4, l5, l6, l7, l8, l9, l10, l11]):
        sent(landing, landing.shape[0], send_sem.at[i])


def per_device(
    tokens,
    attn_gain,
    mlp_gain,
    w_query,
    w_key,
    w_value,
    w_out,
    w_gate,
    w_up,
    w_down,
    cache_keys,
    cache_values,
    slot_owner,
    slot_fill,
):
    n = lax.axis_size("req")
    m = lax.axis_size("kv")

    def padded(row):
        return jnp.pad(row.astype(F32).reshape(n, 64), ((0, 0), (0, 64)))

    smem = pl.BlockSpec(memory_space=pltpu.SMEM)
    vmem = pl.BlockSpec(memory_space=pltpu.VMEM)
    anywhere = pl.BlockSpec(memory_space=pl.ANY)
    stored = [w_query, w_key, w_value, w_out, w_gate, w_up, w_down, cache_keys, cache_values]
    pairs = [
        ((n, 1, 128), (n, 1, 128)),
        ((n, 1, 768), (n, 1, 768)),
        ((4, 128), (n, 4, 128)),
        ((n, 1, 640), (n, 1, 640)),
        ((1, 512), (n, 1, 512)),
        ((n, 1, 128), (n, 1, 128)),
        ((n, 128), (m, 8, 128)),
        ((1, 640), (n, 1, 640)),
        ((n, 512), (m, 8, 512)),
        ((8, 256), (m, 8, 256)),
        ((n, 1, 512), (n, 1, 512)),
    ]

    def kernel(*refs):
        layer_kernel(n, m, *refs)

    return pl.pallas_call(
        kernel,
        out_shape=jax.ShapeDtypeStruct((1, 512), BF16),
        in_specs=[smem, smem, vmem, vmem, vmem] + [anywhere] * len(stored),
        out_specs=vmem,
        scratch_shapes=[pltpu.VMEM(array.shape, array.dtype) for array in stored]
        + [pltpu.VMEM(shape, F32) for pair in pairs for shape in pair]
        + [
            pltpu.SemaphoreType.DMA((len(stored),)),
            pltpu.SemaphoreType.DMA((len(pairs),)),
            pltpu.SemaphoreType.DMA((len(pairs),)),
        ],
        compiler_params=pltpu.CompilerParams(
            collective_id=0, has_side_effects=True, vmem_limit_bytes=32 << 20
        ),
        name="decode_layer",
    )(
        slot_owner,
        slot_fill,
        padded(tokens),
        padded(attn_gain),
        padded(mlp_gain),
        *stored,
    )


def solution(mesh):
    placed = (
        P("req", None),
        P(),
        P(),
        P("req", "kv"),
        P("req", "kv"),
        P("req", "kv"),
        P("kv", "req"),
        P("kv", "req"),
        P("kv", "req"),
        P("req", "kv"),
        P("req", None, "kv"),
        P("req", None, "kv"),
        P("req"),
        P("req"),
    )
    return jax.shard_map(
        per_device, mesh=mesh, in_specs=placed, out_specs=P("req", "kv"), check_vma=False
    )
```

```python
import jax
import jax.numpy as jnp
from jax import lax
from jax.experimental import pallas as pl
from jax.experimental.pallas import tpu as pltpu
from jax.sharding import PartitionSpec as P

HQ = 32
HK = 8
DH = 128
GROUP = HQ // HK
PAD = 8

EPS = 1e-05
NEG = -1e30
MESH = pl.DeviceIdType.MESH
F32 = jnp.float32
BF16 = jnp.bfloat16


def dot(left, right):
    return jnp.dot(left, right, preferred_element_type=F32)


def exchange_start(axis, me, count, source, landing, send_sem, recv_sem):
    @pl.loop(1, count, unroll=7)
    def _(step):
        peer = lax.rem(me + count - step, count)
        pltpu.make_async_remote_copy(
            src_ref=source(peer),
            dst_ref=landing.at[me],
            send_sem=send_sem,
            recv_sem=recv_sem,
            device_id={axis: peer},
            device_id_type=MESH,
        ).start()

    pltpu.make_async_copy(source(me), landing.at[me], recv_sem).start()


def landed(landing, recv_sem):
    pltpu.make_async_copy(landing, landing, recv_sem).wait()


def sent(landing, count, send_sem):
    view = landing.at[pl.ds(0, count - 1)]
    pltpu.make_async_copy(view, view, send_sem).wait()


def dot_stored(left, right):
    return lax.dot_general(left, right, (((1,), (1,)), ((), ())), preferred_element_type=F32)


def one_row(block):
    return jnp.concatenate([block[i] for i in range(block.shape[0])], axis=1)


def layer_kernel(
    req_count,
    kv_count,
    owner_ref,
    fill_ref,
    tok_ref,
    again_ref,
    mgain_ref,
    wq_hbm,
    wk_hbm,
    wv_hbm,
    wo_hbm,
    wg_hbm,
    wu_hbm,
    wd_hbm,
    keys_hbm,
    values_hbm,
    out_ref,
    wq,
    wk,
    wv,
    wo,
    wg,
    wu,
    wd,
    keys,
    values,
    s1,
    l1,
    s2,
    l2,
    s3,
    l3,
    s4,
    l4,
    s5,
    l5,
    s6,
    l6,
    s7,
    l7,
    s8,
    l8,
    s9,
    l9,
    s10,
    l10,
    s11,
    l11,
    load_sem,
    send_sem,
    recv_sem,
):
    req = lax.axis_index("req")
    kv = lax.axis_index("kv")
    slots = keys.shape[0]
    block_len = keys.shape[1]
    scale = DH ** (-0.5)
    features = req_count * 64

    barrier = pltpu.get_barrier_semaphore()

    @pl.loop(1, req_count)
    def _(step):
        pl.semaphore_signal(
            barrier,
            inc=1,
            device_id={"req": lax.rem(req + step, req_count)},
            device_id_type=MESH,
        )

    @pl.loop(1, kv_count)
    def _(step):
        pl.semaphore_signal(
            barrier,
            inc=1,
            device_id={"kv": lax.rem(kv + step, kv_count)},
            device_id_type=MESH,
        )

    loads = [
        pltpu.make_async_copy(source, target, load_sem.at[i])
        for i, (source, target) in enumerate(
            [
                (wq_hbm, wq),
                (wk_hbm, wk),
                (wv_hbm, wv),
                (keys_hbm, keys),
                (values_hbm, values),
                (wo_hbm, wo),
                (wg_hbm, wg),
                (wu_hbm, wu),
                (wd_hbm, wd),
            ]
        )
    ]
    for load in loads:
        load.start()

    def req_start(i, source, landing):
        exchange_start("req", req, req_count, source, landing, send_sem.at[i], recv_sem.at[i])

    def kv_start(i, source, landing):
        exchange_start("kv", kv, kv_count, source, landing, send_sem.at[i], recv_sem.at[i])

    def kv_rows(array):
        return lambda peer: array.at[pl.ds(pl.multiple_of(peer * 8, 8), 8)]

    tok = tok_ref[...]
    mean = jnp.sum(jnp.sum(tok * tok, axis=0), axis=1, keepdims=True) / features
    s1[...] = (tok * lax.rsqrt(mean + EPS) * again_ref[...]).astype(BF16).astype(F32)
    odd = jnp.full((1, 128), lax.rem(req, 2), jnp.int32) == 1

    pl.semaphore_wait(barrier, req_count - 1 + kv_count - 1)

    req_start(0, lambda peer: s1.at[peer // 2], l1)
    for load in loads[:3]:
        load.wait()
    landed(l1, recv_sem.at[0])
    columns = l1[:, 0, :]
    columns = jnp.where(odd, pltpu.roll(columns, 64, 1), columns)[:, :64].astype(BF16)
    width_q = wq.shape[1]
    s2[:, 0, :] = jnp.concatenate(
        [dot(columns, wq[...]), dot(columns, wk[...]), dot(columns, wv[...])], axis=1
    )
    req_start(1, lambda peer: s2.at[peer], l2)
    landed(l2, recv_sem.at[1])
    projected = jnp.sum(l2[...], axis=0).astype(BF16).astype(F32)
    own_query = [projected[:, g * DH : (g + 1) * DH] for g in range(GROUP)]
    new_key = projected[:, width_q : width_q + DH]
    new_value = projected[:, width_q + DH : width_q + 2 * DH]
    s3[...] = jnp.concatenate(own_query, axis=0).astype(BF16)
    req_start(2, lambda peer: s3, l3)
    for load in loads[3:5]:
        load.wait()
    landed(l3, recv_sem.at[2])

    pos = lax.broadcasted_iota(jnp.int32, (PAD, block_len), 1)
    scores = []
    valid = []
    lane = lax.broadcasted_iota(jnp.int32, (1, slots * PAD), 1)
    slot_key = jnp.zeros((1, slots * PAD), jnp.int32)
    for s in range(slots):
        query = l3[owner_ref[s]].astype(F32)
        query = jnp.concatenate([query, jnp.zeros((PAD - GROUP, DH), F32)], axis=0).astype(BF16)
        scores.append(dot_stored(query, keys[s]))
        valid.append(jnp.where(pos < fill_ref[s], 1.0, 0.0))
        slot_key = jnp.where(lane // PAD == s, owner_ref[s], slot_key)
    valid = jnp.concatenate(valid, axis=0) > 0.5
    masked = jnp.where(valid, jnp.concatenate(scores, axis=0) * scale, NEG)
    slot_max = jnp.max(masked, axis=1, keepdims=True)
    prob = jnp.where(valid, jnp.exp(masked - slot_max), 0.0)
    slot_total = jnp.sum(prob, axis=1, keepdims=True)
    prob_low = prob.astype(BF16)
    slot_acc = jnp.concatenate(
        [dot(prob_low[s * PAD : (s + 1) * PAD], values[s]) for s in range(slots)], axis=0
    )
    rows = slots * PAD
    slot_side = jnp.concatenate([slot_acc, jnp.broadcast_to(slot_total, (rows, DH))], axis=1)
    max_lane = jnp.transpose(jnp.broadcast_to(slot_max, (rows, rows)))[0:1]
    request = lax.broadcasted_iota(jnp.int32, (req_count, rows), 0)
    extra_lane = lax.broadcasted_iota(jnp.int32, (req_count, DH), 1)
    extra = jnp.zeros((req_count, DH), F32)
    for g in range(GROUP):
        mine = (request == slot_key) & (lane % PAD == g)
        part_max = jnp.max(jnp.where(mine, max_lane, NEG), axis=1, keepdims=True)
        weight = jnp.where(mine, jnp.exp(jnp.where(mine, max_lane, NEG) - part_max), 0.0)
        part = jnp.dot(
            weight, slot_side, preferred_element_type=F32, precision=lax.Precision.HIGHEST
        )
        s4[:, 0, g * DH : (g + 1) * DH] = part[:, :DH]
        extra = jnp.where(extra_lane == 2 * g, part[:, DH:], extra)
        extra = jnp.where(extra_lane == 2 * g + 1, part_max, extra)
    s4[:, 0, GROUP * DH :] = extra
    req_start(3, lambda peer: s4.at[peer], l4)
    landed(l4, recv_sem.at[3])

    extra = l4[:, 0, GROUP * DH :]
    own_heads = []
    for g in range(GROUP):
        part_total = extra[:, 2 * g : 2 * g + 1]
        part_max = extra[:, 2 * g + 1 : 2 * g + 2]
        run_max = jnp.max(part_max, axis=0, keepdims=True)
        share = jnp.exp(part_max - run_max)
        run_total = jnp.sum(part_total * share, axis=0, keepdims=True)
        run_acc = jnp.sum(l4[:, 0, g * DH : (g + 1) * DH] * share, axis=0, keepdims=True)
        own_score = jnp.sum(own_query[g] * new_key, axis=1, keepdims=True) * scale
        highest = jnp.maximum(run_max, own_score)
        older = jnp.exp(run_max - highest)
        fresh = jnp.exp(own_score - highest)
        total = run_total * older + fresh
        heads = (run_acc * older + fresh * new_value) / total
        own_heads.append(heads)
    s5[...] = jnp.concatenate(own_heads, axis=0).astype(BF16)
    req_start(4, lambda peer: s5, l5)
    loads[5].wait()
    landed(l5, recv_sem.at[4])

    every = l5[...].astype(F32)
    every = jnp.concatenate([every[:, g, :] for g in range(GROUP)], axis=1).astype(BF16)
    out_part = jnp.concatenate([dot_stored(every, wo[...]), jnp.zeros((req_count, 64), F32)], axis=1)
    s6[:, 0, :] = jnp.where(odd, pltpu.roll(out_part, 64, 1), out_part)
    req_start(5, lambda peer: s6.at[peer], l6)
    landed(l6, recv_sem.at[5])
    both = l6[...].reshape(req_count // 2, 2, 1, 128)
    s7[...] = both[:, 0] + both[:, 1]
    kv_start(6, lambda peer: s7.at[pl.ds(peer * 4, 4)], l7)
    landed(l7, recv_sem.at[6])
    block = pl.ds(kv * 4, 4)
    resid = tok_ref[block] + jnp.sum(l7[...], axis=0)
    squares = jnp.sum(jnp.sum(resid * resid, axis=0), axis=1, keepdims=True)
    resid_row = one_row(resid)
    s8[:, :512] = one_row(resid * mgain_ref[block])
    s8[:, 512:] = jnp.broadcast_to(squares, (1, 128))
    req_start(7, lambda peer: s8, l8)
    for load in loads[6:8]:
        load.wait()
    landed(l8, recv_sem.at[7])

    scaled = l8[:, 0, :512].astype(BF16)
    width = wg.shape[0]
    s9[:, 128:256] = l8[:, 0, 512:]
    s9[:, :width] = dot_stored(scaled, wg[...])
    s9[:, 384:512] = jnp.zeros((req_count, 128), F32)
    s9[:, 256 : 256 + width] = dot_stored(scaled, wu[...])
    kv_start(8, kv_rows(s9), l9)
    landed(l9, recv_sem.at[8])
    both = jnp.sum(l9[...], axis=0)
    factor = lax.rsqrt(both[:, 255:256] / features + EPS)
    gate = both[:, :256] * factor
    up = both[:, 256:] * factor
    hidden = (gate / (1.0 + jnp.exp(-gate)) * up).astype(BF16).astype(F32)
    s10[...] = hidden
    kv_start(9, lambda peer: s10, l10)
    loads[8].wait()
    landed(l10, recv_sem.at[9])
    units = l10[...].reshape(req_count, 256)[:, :width].astype(BF16)
    s11[:, 0, :] = dot(units, wd[...])
    req_start(10, lambda peer: s11.at[peer], l11)
    landed(l11, recv_sem.at[10])
    out_ref[...] = (resid_row + jnp.sum(l11[...], axis=0)).astype(BF16)

    for i, landing in enumerate([l1, l2, l3, l4, l5, l6, l7, l8, l9, l10, l11]):
        sent(landing, landing.shape[0], send_sem.at[i])


def per_device(
    tokens,
    attn_gain,
    mlp_gain,
    w_query,
    w_key,
    w_value,
    w_out,
    w_gate,
    w_up,
    w_down,
    cache_keys,
    cache_values,
    slot_owner,
    slot_fill,
):
    n = lax.axis_size("req")
    m = lax.axis_size("kv")

    def in_rows(row):
        return row.astype(F32).reshape(n // 2, 1, 128)

    smem = pl.BlockSpec(memory_space=pltpu.SMEM)
    vmem = pl.BlockSpec(memory_space=pltpu.VMEM)
    anywhere = pl.BlockSpec(memory_space=pl.ANY)
    stored = [w_query, w_key, w_value, w_out.T, w_gate.T, w_up.T, w_down, cache_keys, cache_values]
    pairs = [
        ((n // 2, 1, 128), (n, 1, 128)),
        ((n, 1, 768), (n, 1, 768)),
        ((4, 128), (n, 4, 128)),
        ((n, 1, 640), (n, 1, 640)),
        ((4, 128), (n, 4, 128)),
        ((n, 1, 128), (n, 1, 128)),
        ((n // 2, 1, 128), (m, 4, 1, 128)),
        ((1, 640), (n, 1, 640)),
        ((n, 512), (m, 8, 512)),
        ((8, 256), (m, 8, 256)),
        ((n, 1, 512), (n, 1, 512)),
    ]

    def kernel(*refs):
        layer_kernel(n, m, *refs)

    return pl.pallas_call(
        kernel,
        out_shape=jax.ShapeDtypeStruct((1, 512), BF16),
        in_specs=[smem, smem, vmem, vmem, vmem] + [anywhere] * len(stored),
        out_specs=vmem,
        scratch_shapes=[pltpu.VMEM(array.shape, array.dtype) for array in stored]
        + [pltpu.VMEM(s, BF16 if s[-2:] == (4, 128) else F32) for pair in pairs for s in pair]
        + [
            pltpu.SemaphoreType.DMA((len(stored),)),
            pltpu.SemaphoreType.DMA((len(pairs),)),
            pltpu.SemaphoreType.DMA((len(pairs),)),
        ],
        compiler_params=pltpu.CompilerParams(
            collective_id=0, has_side_effects=True
        ),
        name="decode_layer",
    )(
        slot_owner,
        slot_fill,
        in_rows(tokens),
        in_rows(attn_gain),
        in_rows(mlp_gain),
        *stored,
    )


def solution(mesh):
    placed = (
        P("req", None),
        P(),
        P(),
        P("req", "kv"),
        P("req", "kv"),
        P("req", "kv"),
        P("kv", "req"),
        P("kv", "req"),
        P("kv", "req"),
        P("req", "kv"),
        P("req", None, "kv"),
        P("req", None, "kv"),
        P("req"),
        P("req"),
    )
    return jax.shard_map(
        per_device, mesh=mesh, in_specs=placed, out_specs=P("req", "kv"), check_vma=False
    )
```

```python
import jax
import jax.numpy as jnp
from jax import lax
from jax.experimental import pallas as pl
from jax.experimental.pallas import tpu as pltpu
from jax.sharding import PartitionSpec as P

HQ = 32
HK = 8
DH = 128
GROUP = HQ // HK
PAD = 8

EPS = 1e-05
NEG = -1e30
MESH = pl.DeviceIdType.MESH
F32 = jnp.float32
BF16 = jnp.bfloat16


def dot(left, right):
    return jnp.dot(left, right, preferred_element_type=F32)


def exchange_start(axis, me, count, source, landing, send_sem, recv_sem):
    @pl.loop(1, count, unroll=7)
    def _(step):
        peer = lax.rem(me + count - step, count)
        pltpu.make_async_remote_copy(
            src_ref=source(peer),
            dst_ref=landing.at[me],
            send_sem=send_sem,
            recv_sem=recv_sem,
            device_id={axis: peer},
            device_id_type=MESH,
        ).start()

    pltpu.make_async_copy(source(me), landing.at[me], recv_sem).start()


def landed(landing, recv_sem):
    pltpu.make_async_copy(landing, landing, recv_sem).wait()


def sent(landing, count, send_sem):
    view = landing.at[pl.ds(0, count - 1)]
    pltpu.make_async_copy(view, view, send_sem).wait()


def dot_stored(left, right):
    return lax.dot_general(left, right, (((1,), (1,)), ((), ())), preferred_element_type=F32)


def one_row(block):
    return jnp.concatenate([block[i] for i in range(block.shape[0])], axis=1)


def layer_kernel(
    req_count,
    kv_count,
    owner_ref,
    fill_ref,
    tok_ref,
    again_ref,
    mgain_ref,
    wq_hbm,
    wk_hbm,
    wv_hbm,
    wo_hbm,
    wg_hbm,
    wu_hbm,
    wd_hbm,
    keys_hbm,
    values_hbm,
    out_ref,
    wq,
    wk,
    wv,
    wo,
    wg,
    wu,
    wd,
    keys,
    values,
    s1,
    l1,
    s2,
    l2,
    s3,
    l3,
    s4,
    l4,
    s5,
    l5,
    s6,
    l6,
    s7,
    l7,
    s8,
    l8,
    s9,
    l9,
    s10,
    l10,
    s11,
    l11,
    t9,
    load_sem,
    send_sem,
    recv_sem,
):
    req = lax.axis_index("req")
    kv = lax.axis_index("kv")
    slots = keys.shape[0]
    block_len = keys.shape[1]
    scale = DH ** (-0.5)
    features = req_count * 64

    barrier = pltpu.get_barrier_semaphore()

    @pl.loop(1, req_count, unroll=7)
    def _(step):
        pl.semaphore_signal(
            barrier,
            inc=1,
            device_id={"req": lax.rem(req + step, req_count)},
            device_id_type=MESH,
        )

    @pl.loop(1, kv_count)
    def _(step):
        pl.semaphore_signal(
            barrier,
            inc=1,
            device_id={"kv": lax.rem(kv + step, kv_count)},
            device_id_type=MESH,
        )

    loads = [
        pltpu.make_async_copy(source, target, load_sem.at[i])
        for i, (source, target) in enumerate(
            [
                (wq_hbm, wq),
                (wk_hbm, wk),
                (wv_hbm, wv),
                (keys_hbm, keys),
                (values_hbm, values),
                (wo_hbm, wo),
                (wg_hbm, wg),
                (wu_hbm, wu),
                (wd_hbm, wd),
            ]
        )
    ]
    for load in loads:
        load.start()

    def req_start(i, source, landing):
        exchange_start("req", req, req_count, source, landing, send_sem.at[i], recv_sem.at[i])

    def kv_start(i, source, landing):
        exchange_start("kv", kv, kv_count, source, landing, send_sem.at[i], recv_sem.at[i])

    tok = tok_ref[...]
    mean = jnp.sum(jnp.sum(tok * tok, axis=0), axis=1, keepdims=True) / features
    s1[...] = (tok * lax.rsqrt(mean + EPS) * again_ref[...]).astype(BF16).astype(F32)
    odd = jnp.full((1, 128), lax.rem(req, 2), jnp.int32) == 1

    pl.semaphore_wait(barrier, req_count - 1 + kv_count - 1)

    req_start(0, lambda peer: s1.at[peer // 2], l1)
    for load in loads[:3]:
        load.wait()
    landed(l1, recv_sem.at[0])
    columns = l1[:, 0, :]
    columns = jnp.where(odd, pltpu.roll(columns, 64, 1), columns)[:, :64].astype(BF16)
    width_q = wq.shape[1]
    s2[:, 0, :] = jnp.concatenate(
        [dot(columns, wq[...]), dot(columns, wk[...]), dot(columns, wv[...])], axis=1
    )
    req_start(1, lambda peer: s2.at[peer], l2)
    landed(l2, recv_sem.at[1])
    projected = jnp.sum(l2[...], axis=0).astype(BF16).astype(F32)
    own_query = [projected[:, g * DH : (g + 1) * DH] for g in range(GROUP)]
    new_key = projected[:, width_q : width_q + DH]
    new_value = projected[:, width_q + DH : width_q + 2 * DH]
    s3[...] = jnp.concatenate(own_query, axis=0).astype(BF16)
    req_start(2, lambda peer: s3, l3)
    for load in loads[3:5]:
        load.wait()
    landed(l3, recv_sem.at[2])

    pos = lax.broadcasted_iota(jnp.int32, (PAD, block_len), 1)
    scores = []
    valid = []
    lane = lax.broadcasted_iota(jnp.int32, (1, slots * PAD), 1)
    slot_key = jnp.zeros((1, slots * PAD), jnp.int32)
    for s in range(slots):
        query = l3[owner_ref[s]].astype(F32)
        query = jnp.concatenate([query, jnp.zeros((PAD - GROUP, DH), F32)], axis=0).astype(BF16)
        scores.append(dot_stored(query, keys[s]))
        valid.append(jnp.where(pos < fill_ref[s], 1.0, 0.0))
        slot_key = jnp.where(lane // PAD == s, owner_ref[s], slot_key)
    valid = jnp.concatenate(valid, axis=0) > 0.5
    masked = jnp.where(valid, jnp.concatenate(scores, axis=0) * scale, NEG)
    slot_max = jnp.max(masked, axis=1, keepdims=True)
    prob = jnp.where(valid, jnp.exp(masked - slot_max), 0.0)
    slot_total = jnp.sum(prob, axis=1, keepdims=True)
    prob_low = prob.astype(BF16)
    slot_acc = jnp.concatenate(
        [dot(prob_low[s * PAD : (s + 1) * PAD], values[s]) for s in range(slots)], axis=0
    )
    rows = slots * PAD
    slot_side = jnp.concatenate([slot_acc, jnp.broadcast_to(slot_total, (rows, DH))], axis=1)
    max_lane = jnp.transpose(jnp.broadcast_to(slot_max, (rows, rows)))[0:1]
    request = lax.broadcasted_iota(jnp.int32, (req_count, rows), 0)
    extra_lane = lax.broadcasted_iota(jnp.int32, (req_count, DH), 1)
    extra = jnp.zeros((req_count, DH), F32)
    for g in range(GROUP):
        mine = (request == slot_key) & (lane % PAD == g)
        part_max = jnp.max(jnp.where(mine, max_lane, NEG), axis=1, keepdims=True)
        weight = jnp.where(mine, jnp.exp(jnp.where(mine, max_lane, NEG) - part_max), 0.0)
        part = jnp.dot(
            weight, slot_side, preferred_element_type=F32, precision=lax.Precision.HIGHEST
        )
        s4[:, 0, g * DH : (g + 1) * DH] = part[:, :DH]
        extra = jnp.where(extra_lane == 2 * g, part[:, DH:], extra)
        extra = jnp.where(extra_lane == 2 * g + 1, part_max, extra)
    s4[:, 0, GROUP * DH :] = extra
    req_start(3, lambda peer: s4.at[peer], l4)
    landed(l4, recv_sem.at[3])

    extra = l4[:, 0, GROUP * DH :]
    own_heads = []
    for g in range(GROUP):
        part_total = extra[:, 2 * g : 2 * g + 1]
        part_max = extra[:, 2 * g + 1 : 2 * g + 2]
        run_max = jnp.max(part_max, axis=0, keepdims=True)
        share = jnp.exp(part_max - run_max)
        run_total = jnp.sum(part_total * share, axis=0, keepdims=True)
        run_acc = jnp.sum(l4[:, 0, g * DH : (g + 1) * DH] * share, axis=0, keepdims=True)
        own_score = jnp.sum(own_query[g] * new_key, axis=1, keepdims=True) * scale
        highest = jnp.maximum(run_max, own_score)
        older = jnp.exp(run_max - highest)
        fresh = jnp.exp(own_score - highest)
        total = run_total * older + fresh
        heads = (run_acc * older + fresh * new_value) / total
        own_heads.append(heads)
    s5[...] = jnp.concatenate(own_heads, axis=0).astype(BF16)
    req_start(4, lambda peer: s5, l5)
    loads[5].wait()
    landed(l5, recv_sem.at[4])

    every = l5[...].astype(F32)
    every = jnp.concatenate([every[:, g, :] for g in range(GROUP)], axis=1).astype(BF16)
    out_part = jnp.concatenate([dot_stored(every, wo[...]), jnp.zeros((req_count, 64), F32)], axis=1)
    s6[:, 0, :] = jnp.where(odd, pltpu.roll(out_part, 64, 1), out_part)
    req_start(5, lambda peer: s6.at[peer], l6)
    landed(l6, recv_sem.at[5])
    both = l6[...].reshape(req_count // 2, 2, 1, 128)
    s7[...] = both[:, 0] + both[:, 1]
    kv_start(6, lambda peer: s7.at[pl.ds(peer * 4, 4)], l7)
    landed(l7, recv_sem.at[6])
    block = pl.ds(kv * 4, 4)
    resid = tok_ref[block] + jnp.sum(l7[...], axis=0)
    resid_row = one_row(resid)
    gained = resid * mgain_ref[block]
    s8[...] = jnp.concatenate([gained[i] for i in range(4)], axis=0).astype(BF16)
    inverse = one_row(1.0 / mgain_ref[block])
    req_start(7, lambda peer: s8, l8)
    for load in loads[6:8]:
        load.wait()
    landed(l8, recv_sem.at[7])

    every = l8[...].astype(F32)
    every = jnp.concatenate([every[:, i, :] for i in range(4)], axis=1)
    scaled = every.astype(BF16)
    plain = every * inverse
    squares = jnp.sum(plain * plain, axis=1, keepdims=True)
    high = squares.astype(BF16).astype(F32)
    first = lax.broadcasted_iota(jnp.int32, (req_count, 128), 1) < 112
    width = wg.shape[0]
    t9[:, 128:256] = jnp.where(first, high, squares - high)
    t9[:, :width] = dot_stored(scaled, wg[...])
    t9[:, 384:512] = jnp.zeros((req_count, 128), F32)
    t9[:, 256 : 256 + width] = dot_stored(scaled, wu[...])
    s9[...] = t9[...].reshape(kv_count, 8, 512).astype(BF16)
    kv_start(8, lambda peer: s9.at[peer], l9)
    landed(l9, recv_sem.at[8])
    both = jnp.sum(l9[...].astype(F32), axis=0)
    squares = both[:, 224:225] + both[:, 255:256]
    factor = lax.rsqrt(squares / features + EPS)
    gate = both[:, :256] * factor
    up = both[:, 256:] * factor
    s10[...] = (gate / (1.0 + jnp.exp(-gate)) * up).astype(BF16)
    kv_start(9, lambda peer: s10, l10)
    loads[8].wait()
    landed(l10, recv_sem.at[9])
    units = l10[...].astype(F32).reshape(req_count, 256)[:, :width].astype(BF16)
    down = dot(units, wd[...])
    s11[...] = jnp.stack([down[:, i * 128 : (i + 1) * 128] for i in range(4)], axis=1).astype(BF16)
    req_start(10, lambda peer: s11.at[peer], l11)
    landed(l11, recv_sem.at[10])
    down = jnp.sum(l11[...].astype(F32), axis=0)
    down = jnp.concatenate([down[i : i + 1] for i in range(4)], axis=1)
    out_ref[...] = (resid_row + down).astype(BF16)

    for i, landing in enumerate([l1, l2, l3, l4, l5, l6, l7, l8, l9, l10, l11]):
        sent(landing, landing.shape[0], send_sem.at[i])


def per_device(
    tokens,
    attn_gain,
    mlp_gain,
    w_query,
    w_key,
    w_value,
    w_out,
    w_gate,
    w_up,
    w_down,
    cache_keys,
    cache_values,
    slot_owner,
    slot_fill,
):
    n = lax.axis_size("req")
    m = lax.axis_size("kv")

    def in_rows(row):
        return row.astype(F32).reshape(n // 2, 1, 128)

    smem = pl.BlockSpec(memory_space=pltpu.SMEM)
    vmem = pl.BlockSpec(memory_space=pltpu.VMEM)
    anywhere = pl.BlockSpec(memory_space=pl.ANY)
    stored = [w_query, w_key, w_value, w_out.T, w_gate.T, w_up.T, w_down, cache_keys, cache_values]
    pairs = [
        ((n // 2, 1, 128), (n, 1, 128)),
        ((n, 1, 768), (n, 1, 768)),
        ((4, 128), (n, 4, 128)),
        ((n, 1, 640), (n, 1, 640)),
        ((4, 128), (n, 4, 128)),
        ((n, 1, 128), (n, 1, 128)),
        ((n // 2, 1, 128), (m, 4, 1, 128)),
        ((4, 128), (n, 4, 128)),
        ((m, 8, 512), (m, 8, 512)),
        ((8, 256), (m, 8, 256)),
        ((n, 4, 128), (n, 4, 128)),
    ]

    low = ((4, 128), (8, 512), (8, 256))

    def kernel(*refs):
        layer_kernel(n, m, *refs)

    return pl.pallas_call(
        kernel,
        out_shape=jax.ShapeDtypeStruct((1, 512), BF16),
        in_specs=[smem, smem, vmem, vmem, vmem] + [anywhere] * len(stored),
        out_specs=vmem,
        scratch_shapes=[pltpu.VMEM(array.shape, array.dtype) for array in stored]
        + [pltpu.VMEM(s, BF16 if s[-2:] in low else F32) for pair in pairs for s in pair]
        + [
            pltpu.VMEM((n, 512), F32),
            pltpu.SemaphoreType.DMA((len(stored),)),
            pltpu.SemaphoreType.DMA((len(pairs),)),
            pltpu.SemaphoreType.DMA((len(pairs),)),
        ],
        compiler_params=pltpu.CompilerParams(
            collective_id=0, has_side_effects=True
        ),
        name="decode_layer",
    )(
        slot_owner,
        slot_fill,
        in_rows(tokens),
        in_rows(attn_gain),
        in_rows(mlp_gain),
        *stored,
    )


def solution(mesh):
    placed = (
        P("req", None),
        P(),
        P(),
        P("req", "kv"),
        P("req", "kv"),
        P("req", "kv"),
        P("kv", "req"),
        P("kv", "req"),
        P("kv", "req"),
        P("req", "kv"),
        P("req", None, "kv"),
        P("req", None, "kv"),
        P("req"),
        P("req"),
    )
    return jax.shard_map(
        per_device, mesh=mesh, in_specs=placed, out_specs=P("req", "kv"), check_vma=False
    )
```
